32 devices in a mesh: row: 4 (over y, core), col: 8 (over z, x).
Axes of the slice: x: 2, y: 2, z: 4, core: 2. Of those that a mesh axis runs over, the one named last changes fastest.
Arguments:
- z_real: float32 [3, 3072, 3072], P(None, 'col', 'row'), may hold values from -4 to 4, as said below
- z_imag: float32 [3, 3072, 3072], P(None, 'col', 'row'), may hold values from -4 to 4, as said below
- rotation: float32 [3072, 3072], P('col', 'row'), may hold values from -2 to 2
Outputs:
- gradient: float32 [3072, 3072], P('col', 'row')
- diagonals: float32 [3, 2, 3072], P(None, None, 'row')
The draws below stay inside these ranges and needn't reach their ends.
Inputs may be any that keep to these rules, and one draw needn't show every extreme that they name: Each Z_i is symmetric: z_real[i] and z_imag[i] equal their transposes. `z_imag`: symmetric in the last two dimensions, like z_real.
All inputs are finite; a program needn't handle non-finite values.
Results may differ from the reference program's by a relative error of at most 0.00018.
Values sent between devices are 32-bit elements; how exact they have to be, the bound alone decides.
No kernel may reach another device: no remote copies, remote signals or barrier semaphores. Data moves between devices by JAX's collectives and lax.ppermute only.
A program may use at most 128 MiB of HBM per device.

```python
import jax
import jax.numpy as jnp
from jax import lax

N = 3072
DIRS = 3


def symmetric_part(key):
    noise = jax.random.normal(key, (DIRS, N, N), jnp.float32)
    noise = noise / jnp.sqrt(jnp.float32(N))
    return (noise + jnp.swapaxes(noise, 1, 2)) * 0.70710678


def diagonal_part(key):
    phases = jax.random.uniform(jax.random.fold_in(key, 11), (DIRS, N), jnp.float32, -3.14159265, 3.14159265)
    amplitude = jax.random.uniform(jax.random.fold_in(key, 12), (DIRS, N), jnp.float32, 0.3, 1.0)
    return (amplitude * jnp.cos(phases), amplitude * jnp.sin(phases))


def draw_z_real(key, part):
    cosine, sine = diagonal_part(key)
    eye = jnp.eye(N, dtype=jnp.float32)
    return symmetric_part(jax.random.fold_in(key, 21)) + cosine[:, :, None] * eye[None]


def draw_z_imag(key, part):
    cosine, sine = diagonal_part(key)
    eye = jnp.eye(N, dtype=jnp.float32)
    return symmetric_part(jax.random.fold_in(key, 22)) + sine[:, :, None] * eye[None]


def draw_rotation(key, part):
    inner = jax.random.fold_in(key, 31)
    noise = jax.random.normal(inner, (N, N), jnp.float32)
    return 0.8 * jnp.eye(N, dtype=jnp.float32) + 0.6 * noise / jnp.sqrt(jnp.float32(N))


def setup_inputs(seed: int = 0) -> dict:
    key_list = jax.random.split(jax.random.key(seed), 4)
    return {
        "z_real": draw_z_real(jax.random.fold_in(key_list[3], 71), 0),
        "z_imag": draw_z_imag(jax.random.fold_in(key_list[3], 71), 0),
        "rotation": draw_rotation(jax.random.fold_in(key_list[3], 71), 0),
    }


def reference(z_real, z_imag, rotation):
    highest = lax.Precision.HIGHEST
    gradient = jnp.zeros((N, N), jnp.float32)
    rows = []
    for direc in range(DIRS):
        real_part = jnp.dot(z_real[direc], rotation, precision=highest, preferred_element_type=jnp.float32)
        imag_part = jnp.dot(z_imag[direc], rotation, precision=highest, preferred_element_type=jnp.float32)
        diag_real = jnp.sum(rotation * real_part, axis=0)
        diag_imag = jnp.sum(rotation * imag_part, axis=0)
        rows.append(jnp.stack([diag_real, diag_imag]))
        gradient = gradient + real_part * diag_real[None, :] + imag_part * diag_imag[None, :]
    return 4.0 * gradient, jnp.stack(rows)
```

```python
import functools

import jax
import jax.numpy as jnp
from jax import lax
from jax.experimental import pallas as pl
from jax.experimental.pallas import tpu as pltpu
from jax.sharding import PartitionSpec as P

AXES = ("row", "col")
INTERPRET = False


def gathered(z_real, z_imag, rotation):
    highest = lax.Precision.HIGHEST
    count = z_real.shape[0]
    full = [lax.all_gather(z, "row", axis=2, tiled=True) for z in (z_real, z_imag)]
    u_columns = lax.all_gather(rotation, "col", axis=0, tiled=True)
    products = [[jnp.dot(z[i], u_columns, precision=highest) for z in full] for i in range(count)]
    rows = [jnp.stack([jnp.sum(rotation * p, axis=0) for p in pair]) for pair in products]
    diagonals = lax.psum(jnp.stack(rows), "col")
    gradient = jnp.zeros(rotation.shape, jnp.float32)
    for i in range(count):
        for j in range(2):
            gradient = gradient + products[i][j] * diagonals[i, j][None, :]
    return 4.0 * gradient, diagonals


def permute(x, n_row, n_col, dr, dc):
    pairs = [
        (r * n_col + c, (r ^ dr) * n_col + (c ^ dc)) for r in range(n_row) for c in range(n_col)
    ]
    return lax.ppermute(x, AXES, pairs)


def split(x):
    high = lax.reduce_precision(x, 8, 7)
    return high.astype(jnp.bfloat16), (x - high).astype(jnp.bfloat16)


def product_kernel(off, hi_own, lo_own, hi_par, lo_par, *refs):
    pieces, (v_own, v_other, p_ref, d_ref, u_hi, u_lo) = refs[:8], refs[8:]
    k = pl.program_id(0)
    rows, width = pieces[0].shape

    @pl.when(k == 0)
    def _():
        for side in range(2):
            for q in range(4):
                x = pieces[4 * side + q][...]
                high = x.astype(jnp.bfloat16)
                low = (x - high.astype(jnp.float32)).astype(jnp.bfloat16)
                start = pl.multiple_of(off[q], 128)
                u_hi[pl.ds(start, rows), side * width : (side + 1) * width] = high
                u_lo[pl.ds(start, rows), side * width : (side + 1) * width] = low

    depth = hi_own.shape[2]
    dot = functools.partial(jnp.dot, preferred_element_type=jnp.float32)
    total = dot(hi_own[0], u_lo[:depth]) + dot(hi_par[0], u_lo[depth:])
    total += dot(lo_own[0], u_hi[:depth]) + dot(lo_par[0], u_hi[depth:])
    total += dot(hi_own[0], u_hi[:depth]) + dot(hi_par[0], u_hi[depth:])
    p_ref[0] = total
    d_ref[pl.ds(k, 1), :width] = jnp.sum(total[:, :width] * v_own[...], axis=0, keepdims=True)
    d_ref[pl.ds(k, 1), width:] = jnp.sum(total[:, width:] * v_other[...], axis=0, keepdims=True)


def product(off, z_split, pieces, v_own, v_other):
    count, rows, depth = z_split[0].shape
    width = pieces[0].shape[1]
    z_spec = pl.BlockSpec((1, rows, depth), lambda k, off: (k, 0, 0))
    u_spec = pl.BlockSpec((pieces[0].shape[0], width), lambda k, off: (0, 0))
    v_spec = pl.BlockSpec((rows, width), lambda k, off: (0, 0))
    flops = 6 * count * rows * 2 * depth * 2 * width
    return pl.pallas_call(
        product_kernel,
        out_shape=(
            jax.ShapeDtypeStruct((count, rows, 2 * width), jnp.float32),
            jax.ShapeDtypeStruct((8, 2 * width), jnp.float32),
        ),
        grid_spec=pltpu.PrefetchScalarGridSpec(
            num_scalar_prefetch=1,
            grid=(count,),
            in_specs=[z_spec] * 4 + [u_spec] * 8 + [v_spec] * 2,
            out_specs=(
                pl.BlockSpec((1, rows, 2 * width), lambda k, off: (k, 0, 0)),
                pl.BlockSpec((8, 2 * width), lambda k, off: (0, 0)),
            ),
            scratch_shapes=[pltpu.VMEM((2 * depth, 2 * width), jnp.bfloat16)] * 2,
        ),
        compiler_params=pltpu.CompilerParams(dimension_semantics=("arbitrary",)),
        cost_estimate=pl.CostEstimate(
            flops=flops, bytes_accessed=4 * count * rows * (2 * depth + 2 * width), transcendentals=0
        ),
        interpret=INTERPRET,
    )(off, *z_split, *pieces, v_own, v_other)


def widths_of(columns):
    tiles = columns // 128
    if columns % 128 or tiles < 3:
        return (columns,)
    base, extra = divmod(tiles, 3)
    return tuple(128 * (base + (i < extra)) for i in range(3))


def relayed(n_row, n_col, z_real, z_imag, rotation):
    exchange = functools.partial(permute, n_row=n_row, n_col=n_col)
    row, col = lax.axis_index("row"), lax.axis_index("col")
    y, core, z, x = row // 2, row % 2, col // 2, col % 2
    same = (z // 2) == y
    rows, columns = rotation.shape
    depth = z_real.shape[2]

    own = jnp.concatenate([z_real, z_imag], axis=0)
    partner = jnp.concatenate(
        [exchange(z_real, dr=1, dc=0), exchange(z_imag, dr=1, dc=0)], axis=0
    )
    z_split = (*split(own), *split(partner))
    first = jnp.where((z % 2) == core, 0, 1).astype(jnp.int32)
    x = x.astype(jnp.int32)
    piece = depth // 2
    off = jnp.stack(
        [
            first * depth + x * piece,
            first * depth + (1 - x) * piece,
            (1 - first) * depth + x * piece,
            (1 - first) * depth + (1 - x) * piece,
        ]
    )

    gradients, diagonals, start = [], [], 0
    for width in widths_of(columns):
        u = lax.slice_in_dim(rotation, start, start + width, axis=1)
        start += width
        u_2, u_3, u_1 = exchange(u, dr=0, dc=4), exchange(u, dr=0, dc=6), exchange(u, dr=0, dc=2)
        a_1, a_2 = jnp.where(same, u, u_2), jnp.where(same, u_1, u_3)
        b_1, b_2 = jnp.where(same, u_2, u), jnp.where(same, u_3, u_1)
        xa_1, xa_2 = exchange(a_1, dr=0, dc=1), exchange(a_2, dr=0, dc=1)
        r_1, r_2 = exchange(b_1, dr=2, dc=0), exchange(b_2, dr=2, dc=0)
        xr_1, xr_2 = exchange(r_1, dr=0, dc=1), exchange(r_2, dr=0, dc=1)
        partial, diag = product(off, z_split, (a_1, xa_1, a_2, xa_2, r_1, xr_1, r_2, xr_2), u, r_1)

        diag = jnp.concatenate(
            [
                diag[:, :width] * jnp.where(same, 1.0, 2.0),
                diag[:, width:] * jnp.where(same, 1.0, 0.0),
            ],
            axis=1,
        )
        swap = lambda d: jnp.concatenate([d[:, width:], d[:, :width]], axis=1)
        d_x, d_y, d_xy = (exchange(diag, dr=dr, dc=dc) for dr, dc in ((0, 1), (2, 0), (2, 1)))
        diag = (diag + d_x) + swap(d_y + d_xy)
        d_1, d_2, d_3 = (exchange(diag, dr=0, dc=dc) for dc in (2, 4, 6))
        diag = (diag + d_1) + (d_2 + d_3)

        count = partial.shape[0]
        combined = [
            4.0
            * sum(
                partial[k, :, side * width : (side + 1) * width]
                * diag[k : k + 1, side * width : (side + 1) * width]
                for k in range(count)
            )
            for side in range(2)
        ]
        gradients.append(combined[0] + exchange(combined[1], dr=2, dc=0))
        diagonals.append(diag[:count, :width])
    diagonals = jnp.concatenate(diagonals, axis=1)
    half = diagonals.shape[0] // 2
    return jnp.concatenate(gradients, axis=1), jnp.stack([diagonals[:half], diagonals[half:]], axis=1)


def solution(mesh):
    n_row, n_col = mesh.shape["row"], mesh.shape["col"]
    shards = functools.partial(relayed, n_row, n_col) if (n_row, n_col) == (4, 8) else gathered
    in_specs = (P(None, "col", "row"), P(None, "col", "row"), P("col", "row"))
    out_specs = (P("col", "row"), P(None, None, "row"))
    return jax.shard_map(shards, mesh=mesh, in_specs=in_specs, out_specs=out_specs, check_vma=False)
```
